512 devices in a mesh: dp: 32 (over y, z_hi, core), space: 16 (over x, z_lo).
Axes of the slice: x: 4, y: 8, z: 8 (z_hi: 2, z_lo: 4; z = z_hi * 4 + z_lo), core: 2. Of those that a mesh axis runs over, the one named last changes fastest.
Arguments:
- scenes: bfloat16 [64, 224, 8, 768], P('dp', 'space'), may hold values from -8 to 8
- kernel: bfloat16 [7, 7, 768], replicated, may hold values from -0.875 to 0.875
- weight_in: bfloat16 [768, 1536], replicated, may hold values from -0.21875 to 0.21875
- weight_out: bfloat16 [1536, 768], replicated, may hold values from -0.15625 to 0.15625
- captions: bfloat16 [64, 768], P('dp'), may hold values from -0.21972656 to 0.21972656
- positives: int32 [64], P('dp'), may hold values from 0 to 63, each once
Outputs:
- loss: float32 [], replicated
- text_grad: float32 [64, 768], P('dp')
- kernel_grad: float32 [7, 7, 768], replicated
The draws below stay inside these ranges and needn't reach their ends.
Inputs may be any that keep to these rules, and one draw needn't show every extreme that they name: `positives`: every caption index appears exactly once.
All inputs are finite; a program needn't handle non-finite values.
Results may differ from the reference program's by a relative error of at most 0.0054.
Values may be sent and summed in bfloat16 or wider, within the bound.
A program may use at most 64 MiB of HBM per device.

```python
import jax
import jax.numpy as jnp
from jax import lax

C = 768
HID = 1536
COLS = 8
IMAGES = 64
HEIGHT = 224


def draw_scenes(key, part):
    key_offset = jax.random.fold_in(key, 11)
    key_noise = jax.random.fold_in(key, 12)
    offset = jax.random.normal(key_offset, (IMAGES, 1, 1, C), jnp.float32)
    noise_part = jax.random.normal(key_noise, (IMAGES, HEIGHT, COLS, C), jnp.float32)
    result = noise_part + offset
    return jnp.clip(result, -8.0, 8.0).astype(jnp.bfloat16)


def block_levels(own_key, dims, split, low, high):
    level = 1.0
    for dim, blocks in split:
        steps = jax.random.uniform(jax.random.fold_in(jax.random.fold_in(own_key, 6), dim), (blocks,), jnp.float32, low / len(split), high / len(split))
        level = level * jnp.repeat(jnp.exp(steps), dims[dim] // blocks).reshape((-1,) + (1,) * (len(dims) - 1 - dim))
    return level


def normal_values(stream_key, shape, scale, bound, shards=(), kind=jnp.bfloat16):
    drawn = jax.random.normal(stream_key, shape, jnp.float32) * scale
    if len(shards) > 0:
        drawn = block_levels(stream_key, shape, shards, -0.22, 0.18) * drawn
    return jnp.clip(drawn, min=-bound, max=bound).astype(kind)


def setup_inputs(seed: int = 0) -> dict:
    splits = jax.random.split(jax.random.key(seed), 7)
    scenes = draw_scenes(jax.random.fold_in(splits[6], 71), 0)
    kernel = normal_values(splits[1], (7, 7, C), 49 ** -0.5, 0.875)
    weight_in = normal_values(splits[2], (C, HID), C ** -0.5, 0.21875)
    weight_out = normal_values(splits[3], (HID, C), HID ** -0.5, 0.15625)
    captions = normal_values(splits[4], (IMAGES, C), 0.036, 0.21972656, ((0, 32),))
    positives = jax.random.permutation(splits[5], IMAGES).astype(jnp.int32)
    return {"scenes": scenes, "kernel": kernel, "weight_in": weight_in, "weight_out": weight_out, "captions": captions, "positives": positives}


EPS = 1e-06
LOGIT_SCALE = 10.0
LOGIT_BIAS = -1.0
GELU_C = 0.7978845608028654

def gelu_tanh(values):
    return 0.5 * values * (1.0 + jnp.tanh(GELU_C * (values + 0.044715 * values * values * values)))

def gelu_slope(values):
    tangent = jnp.tanh(GELU_C * (values + 0.044715 * values * values * values))
    return 0.5 * (1.0 + tangent) + 0.5 * values * (1.0 - tangent * tangent) * GELU_C * (1.0 + 3.0 * 0.044715 * values * values)

def depthwise(padded, kernel, tile_rows, tile_cols):
    total = jnp.zeros(padded.shape[:-3] + (tile_rows, tile_cols, padded.shape[-1]), jnp.float32)
    for row_shift in range(7):
        for col_shift in range(7):
            total = total + kernel[row_shift, col_shift].astype(jnp.float32) * padded[..., row_shift:row_shift + tile_rows, col_shift:col_shift + tile_cols, :]
    return total

def kernel_terms(padded, conv_grad, tile_rows, tile_cols):
    summed_axes = tuple(range(conv_grad.ndim - 1))
    listed = []
    for row_shift in range(7):
        for col_shift in range(7):
            window = padded[..., row_shift:row_shift + tile_rows, col_shift:col_shift + tile_cols, :]
            listed.append(lax.optimization_barrier(jnp.sum(window * conv_grad, axis=summed_axes)))
    return jnp.stack(listed).reshape(7, 7, conv_grad.shape[-1])

def normalize_rows(conv_out):
    center = conv_out - lax.optimization_barrier(jnp.mean(conv_out, axis=-1, keepdims=True))
    inv_scale = lax.rsqrt(lax.optimization_barrier(jnp.mean(center * center, axis=-1, keepdims=True)) + EPS)
    return (center * inv_scale, inv_scale)

def one_forward(one_scene, kernel, weight_in, weight_out):
    padded = jnp.pad(one_scene.astype(jnp.float32), ((3, 3), (3, 3), (0, 0)))
    conv_out = depthwise(padded, kernel, HEIGHT, COLS)
    normed, inv_scale = normalize_rows(conv_out)
    flat_rows = normed.reshape(-1, C).astype(jnp.bfloat16)
    hidden = jnp.dot(flat_rows, weight_in, preferred_element_type=jnp.float32)
    activated = gelu_tanh(hidden).astype(jnp.bfloat16)
    mixed_out = jnp.dot(activated, weight_out, preferred_element_type=jnp.float32)
    block_out = one_scene.reshape(-1, C).astype(jnp.float32) + mixed_out
    return lax.optimization_barrier(jnp.sum(block_out, axis=0))

def one_backward(one_scene, slope_row, kernel, weight_in, weight_out):
    padded = jnp.pad(one_scene.astype(jnp.float32), ((3, 3), (3, 3), (0, 0)))
    conv_out = depthwise(padded, kernel, HEIGHT, COLS)
    normed, inv_scale = normalize_rows(conv_out)
    flat_rows = normed.reshape(-1, C).astype(jnp.bfloat16)
    hidden = jnp.dot(flat_rows, weight_in, preferred_element_type=jnp.float32)
    act_grad = jnp.dot(slope_row[None, :], weight_out.T, preferred_element_type=jnp.float32)
    hidden_grad = (act_grad * gelu_slope(hidden)).astype(jnp.bfloat16)
    normed_grad = jnp.dot(hidden_grad, weight_in.T, preferred_element_type=jnp.float32).reshape(HEIGHT, COLS, C)
    conv_grad = inv_scale * (normed_grad - lax.optimization_barrier(jnp.mean(normed_grad, axis=-1, keepdims=True)) - normed * lax.optimization_barrier(jnp.mean(normed_grad * normed, axis=-1, keepdims=True)))
    return kernel_terms(padded, conv_grad, HEIGHT, COLS)

def unit_rows(values):
    norms = jnp.sqrt(lax.optimization_barrier(jnp.sum(values * values, axis=-1, keepdims=True)) + EPS)
    return (values / norms, norms)

def reference(scenes, kernel, weight_in, weight_out, captions, positives):
    pixels = HEIGHT * COLS
    sums = lax.map(lambda one_scene: one_forward(one_scene, kernel, weight_in, weight_out), scenes)
    pooled = sums / pixels
    image_unit, pooled_norm = unit_rows(pooled)
    text_unit, text_norm = unit_rows(captions.astype(jnp.float32))
    image_cast = image_unit.astype(jnp.bfloat16)
    text_cast = text_unit.astype(jnp.bfloat16)
    logits = LOGIT_SCALE * jnp.dot(image_cast, text_cast.T, preferred_element_type=jnp.float32) + LOGIT_BIAS
    labels = jnp.where(positives[:, None] == jnp.arange(IMAGES, dtype=jnp.int32)[None, :], 1.0, -1.0).astype(jnp.float32)
    loss = jnp.sum(jax.nn.softplus(-labels * logits)) / IMAGES
    pair_grad = (-labels * jax.nn.sigmoid(-labels * logits)).astype(jnp.bfloat16)
    image_side = LOGIT_SCALE * jnp.dot(pair_grad, text_cast, preferred_element_type=jnp.float32)
    caption_side = LOGIT_SCALE * jnp.dot(pair_grad.T, image_cast, preferred_element_type=jnp.float32)
    text_grad = (caption_side - text_unit * lax.optimization_barrier(jnp.sum(text_unit * caption_side, axis=-1, keepdims=True))) / text_norm
    pooled_grad = (image_side - image_unit * lax.optimization_barrier(jnp.sum(image_unit * image_side, axis=-1, keepdims=True))) / pooled_norm
    slope = (pooled_grad / pixels).astype(jnp.bfloat16)
    parts = lax.map(lambda paired: one_backward(paired[0], paired[1], kernel, weight_in, weight_out), (scenes, slope))
    kernel_grad = lax.optimization_barrier(jnp.sum(parts, axis=0))
    return (loss, text_grad, kernel_grad)
```

```python
import functools

import jax
import jax.numpy as jnp
from jax import lax
from jax.experimental import pallas as pl
from jax.experimental.pallas import tpu as pltpu
from jax.sharding import PartitionSpec as P

EPS = 1e-06
LOGIT_SCALE = 10.0
LOGIT_BIAS = -1.0
GELU_C = 0.7978845608028654
MESH = pl.DeviceIdType.MESH
F32 = jnp.float32
BF16 = jnp.bfloat16
TAPS = 7
HALF = 3
LANES = 128
HID_BLOCK = 256
ROW_BLOCK = 32


def dot_nt(a, b):
    return lax.dot_general(a, b, (((1,), (1,)), ((), ())), preferred_element_type=F32)


def dot_nn(a, b):
    return lax.dot_general(a, b, (((1,), (0,)), ((), ())), preferred_element_type=F32)


def shift_cols(values, offset):
    if offset == 0:
        return values
    cols = values.shape[1]
    col = lax.broadcasted_iota(jnp.int32, values.shape, 1) + offset
    rolled = pltpu.roll(values, (-offset) % cols, axis=1)
    return jnp.where((col >= 0) & (col < cols), rolled, 0.0)


def wait_bytes(ref, sem):
    pltpu.make_async_copy(ref, ref, sem).wait()


def kernel(
    cfg,
    scenes_ref, kernel_ref, w_in_hbm, w_out_hbm, captions_ref, positives_ref,
    loss_ref, text_grad_ref, kernel_grad_ref,
    xf, kf, halo, co, nb, inv, w_in, w_out, gp, asum, ssum, hg, cg, agrad,
    pool, capbuf, cap64, text64, imgbuf, img64, pos64,
    ksend, krecv, kown, p1, p2, kfull,
    wsem, halo_s, halo_r, sib_s, sib_r, cap_s, cap_r, pool_s, pool_r, img_s, img_r,
    p1_s, p1_r, p2_s, p2_r, p3_s, p3_r,
):
    n_space, n_dp = cfg
    n_grp = n_dp // 2
    images, rows, cols, chan = scenes_ref.shape
    hid = w_in_hbm.shape[1]
    tile_pix = rows * cols
    pixels = rows * n_space * cols
    n_img = images * n_dp
    ctiles = chan // LANES
    half_tiles = ctiles // 2
    chunk = p1.shape[1]
    used = half_tiles * TAPS * TAPS

    dp = lax.axis_index("dp")
    sp = lax.axis_index("space")
    core = lax.rem(dp, 2)
    other = 1 - core
    grp = lax.div(dp, 2)
    sib = 2 * grp + other
    first = sp == 0
    last = sp == n_space - 1

    def space_peer(d):
        return lax.rem(sp + d, n_space)

    def grp_peer(d):
        return lax.rem(grp + d, n_grp)

    barrier = pltpu.get_barrier_semaphore()
    pl.semaphore_signal(barrier, inc=1, device_id=(sib, sp), device_id_type=MESH)

    def greet_space(d, _):
        pl.semaphore_signal(barrier, inc=1, device_id=(dp, space_peer(d)), device_id_type=MESH)
        return 0

    def greet_grp(d, _):
        pl.semaphore_signal(
            barrier, inc=1, device_id=(2 * grp_peer(d) + core, sp), device_id_type=MESH
        )
        return 0

    lax.fori_loop(1, n_space, greet_space, 0)
    lax.fori_loop(1, n_grp, greet_grp, 0)

    load_in = pltpu.make_async_copy(w_in_hbm, w_in, wsem.at[0])
    load_out = pltpu.make_async_copy(w_out_hbm, w_out, wsem.at[1])
    load_in.start()
    load_out.start()

    kf[...] = kernel_ref[...].astype(F32)
    capbuf[grp, core] = captions_ref[...]

    def conv_tile(ct, _):
        lanes = pl.ds(pl.multiple_of(ct * LANES, LANES), LANES)
        empty = jnp.zeros((HALF, cols, LANES), F32)
        for img in range(images):
            own = scenes_ref[img, :, :, lanes].astype(F32)
            xf[img, HALF : HALF + rows, :, lanes] = own
            ssum[img : img + 1, lanes] = jnp.sum(
                jnp.sum(own, axis=0), axis=0, keepdims=True
            )
            x = jnp.concatenate([empty, own, empty], axis=0)
            total = jnp.zeros((rows, cols, LANES), F32)
            for j in range(TAPS):
                part = jnp.zeros((rows, cols, LANES), F32)
                for i in range(TAPS):
                    part = part + kf[i, j : j + 1, lanes][None] * x[i : i + rows]
                total = total + shift_cols(part, j - HALF)
            co[img * tile_pix : (img + 1) * tile_pix, lanes] = total.reshape(tile_pix, LANES)
        return 0

    lax.fori_loop(0, ctiles, conv_tile, 0)

    pl.semaphore_wait(barrier, n_space + n_grp - 1)

    def halo_copy(src_row, slot, peer):
        return pltpu.make_async_remote_copy(
            src_ref=scenes_ref.at[:, pl.ds(src_row, HALF)],
            dst_ref=halo.at[slot],
            send_sem=halo_s.at[slot],
            recv_sem=halo_r.at[slot],
            device_id=(dp, peer),
            device_id_type=MESH,
        )

    @pl.when(jnp.logical_not(last))
    def _():
        halo_copy(rows - HALF, 0, sp + 1).start()

    @pl.when(jnp.logical_not(first))
    def _():
        halo_copy(0, 1, sp - 1).start()

    @pl.when(first)
    def _():
        halo[0] = jnp.zeros_like(halo[0])

    @pl.when(last)
    def _():
        halo[1] = jnp.zeros_like(halo[1])

    def sib_copy(src, dst, k):
        return pltpu.make_async_remote_copy(
            src_ref=src, dst_ref=dst, send_sem=sib_s.at[k], recv_sem=sib_r.at[k],
            device_id=(sib, sp), device_id_type=MESH,
        )

    def grp_send(ref, send_sem, recv_sem):
        def step(d, _):
            pltpu.make_async_remote_copy(
                src_ref=ref, dst_ref=ref, send_sem=send_sem, recv_sem=recv_sem,
                device_id=(2 * grp_peer(d) + core, sp), device_id_type=MESH,
            ).start()
            return 0

        lax.fori_loop(1, n_grp, step, 0)

    def space_send(ref_of, dst, send_sem, recv_sem):
        def step(d, _):
            peer = space_peer(d)
            pltpu.make_async_remote_copy(
                src_ref=ref_of(peer), dst_ref=dst, send_sem=send_sem, recv_sem=recv_sem,
                device_id=(dp, peer), device_id_type=MESH,
            ).start()
            return 0

        lax.fori_loop(1, n_space, step, 0)

    cap_sib = sib_copy(capbuf.at[grp, core], capbuf.at[grp, core], 0)
    cap_sib.start()
    wait_bytes(capbuf.at[grp, other], sib_r.at[0])
    grp_send(capbuf.at[grp], cap_s, cap_r)

    @pl.when(jnp.logical_not(first))
    def _():
        wait_bytes(halo.at[0], halo_r.at[0])

    @pl.when(jnp.logical_not(last))
    def _():
        wait_bytes(halo.at[1], halo_r.at[1])

    def fix_tile(ct, _):
        lanes = pl.ds(pl.multiple_of(ct * LANES, LANES), LANES)
        pad = jnp.zeros((HALF - 1, cols, LANES), F32)
        for img in range(images):
            before = halo[0, img, :, :, lanes].astype(F32)
            after = halo[1, img, :, :, lanes].astype(F32)
            xf[img, 0:HALF, :, lanes] = before
            xf[img, HALF + rows : 2 * HALF + rows, :, lanes] = after
            xb = jnp.concatenate([before, pad], axis=0)
            xa = jnp.concatenate([pad, after], axis=0)
            tb = jnp.zeros((HALF, cols, LANES), F32)
            ta = jnp.zeros((HALF, cols, LANES), F32)
            for j in range(TAPS):
                pb = jnp.zeros((HALF, cols, LANES), F32)
                pa = jnp.zeros((HALF, cols, LANES), F32)
                for i in range(HALF):
                    pb = pb + kf[i, j : j + 1, lanes][None] * xb[i : i + HALF]
                    pa = pa + kf[i + HALF + 1, j : j + 1, lanes][None] * xa[i : i + HALF]
                tb = tb + shift_cols(pb, j - HALF)
                ta = ta + shift_cols(pa, j - HALF)
            top = img * tile_pix
            low = top + tile_pix - HALF * cols
            co[top : top + HALF * cols, lanes] += tb.reshape(HALF * cols, LANES)
            co[low : low + HALF * cols, lanes] += ta.reshape(HALF * cols, LANES)
        return 0

    lax.fori_loop(0, ctiles, fix_tile, 0)

    def norm_rows(b, _):
        at = pl.ds(pl.multiple_of(b * ROW_BLOCK, ROW_BLOCK), ROW_BLOCK)
        values = co[at, :]
        center = values - jnp.mean(values, axis=-1, keepdims=True)
        scale = lax.rsqrt(jnp.mean(center * center, axis=-1, keepdims=True) + EPS)
        normed = center * scale
        co[at, :] = normed
        nb[at, :] = normed.astype(BF16)
        inv[at, :] = jnp.broadcast_to(scale, (ROW_BLOCK, LANES))
        return 0

    lax.fori_loop(0, images * tile_pix // ROW_BLOCK, norm_rows, 0)

    load_in.wait()

    def hidden_block(n, _):
        at = pl.ds(pl.multiple_of(n * HID_BLOCK, HID_BLOCK), HID_BLOCK)
        h = dot_nn(nb[...], w_in[:, at])
        square = h * h
        tangent = jnp.tanh(GELU_C * (h + 0.044715 * square * h))
        activated = (0.5 * h * (1.0 + tangent)).astype(BF16).astype(F32)
        for img in range(images):
            asum[img : img + 1, at] = jnp.sum(
                activated[img * tile_pix : (img + 1) * tile_pix], axis=0, keepdims=True
            )
        gp[:, at] = 0.5 * (1.0 + tangent) + 0.5 * h * (1.0 - tangent * tangent) * GELU_C * (
            1.0 + 3.0 * 0.044715 * square
        )
        return 0

    asum[...] = jnp.zeros_like(asum)
    lax.fori_loop(0, hid // HID_BLOCK, hidden_block, 0)

    load_out.wait()
    sums = asum[...]
    high = sums.astype(BF16).astype(F32)
    rest = sums - high
    mid = rest.astype(BF16).astype(F32)
    low = rest - mid
    split = jnp.concatenate([high, mid, low], axis=0).astype(BF16)
    mixed = dot_nn(split, w_out[...])
    mixed = mixed[0:8] + mixed[8:16] + mixed[16:24]
    pool[sp] = mixed[0:images] + ssum[...]
    space_send(lambda peer: pool.at[sp], pool.at[sp], pool_s, pool_r)

    wait_bytes(capbuf.at[pl.ds(0, n_grp - 1)], cap_r)
    for g in range(n_grp):
        for c in range(2):
            r = (2 * g + c) * images
            cap64[r : r + images, :] = capbuf[g, c].astype(F32)
    caps = cap64[...]
    caps_norm = jnp.sqrt(jnp.sum(caps * caps, axis=-1, keepdims=True) + EPS)
    text64[...] = (caps / caps_norm).astype(BF16)

    wait_bytes(pool.at[pl.ds(0, n_space - 1)], pool_r)
    pooled = jnp.sum(pool[...], axis=0) / pixels
    pooled_norm = jnp.sqrt(jnp.sum(pooled * pooled, axis=-1, keepdims=True) + EPS)
    image_unit = pooled / pooled_norm
    image_cast = image_unit.astype(BF16)
    row = lax.broadcasted_iota(jnp.int32, (images, LANES), 0)
    own_pos = jnp.where(row == 0, positives_ref[0], positives_ref[1])
    imgbuf[grp, core, :, 0:chan] = image_cast
    imgbuf[grp, core, :, chan:] = own_pos.astype(F32).astype(BF16)
    img_sib = sib_copy(imgbuf.at[grp, core], imgbuf.at[grp, core], 1)
    img_sib.start()

    text_cast = text64[...]
    logits = LOGIT_SCALE * dot_nt(image_cast, text_cast) + LOGIT_BIAS
    col = lax.broadcasted_iota(jnp.int32, (images, n_img), 1)
    labels = jnp.where(own_pos[:, 0:n_img] == col, 1.0, -1.0)
    pair_grad = (-labels * jax.nn.sigmoid(-labels * logits)).astype(BF16)
    image_side = LOGIT_SCALE * dot_nn(pair_grad, text_cast)
    pooled_grad = (
        image_side - image_unit * jnp.sum(image_unit * image_side, axis=-1, keepdims=True)
    ) / pooled_norm
    slope = (pooled_grad / pixels).astype(BF16)
    agrad[...] = dot_nt(slope, w_out[...])

    def grad_block(n, _):
        at = pl.ds(pl.multiple_of(n * HID_BLOCK, HID_BLOCK), HID_BLOCK)
        for img in range(images):
            pix = slice(img * tile_pix, (img + 1) * tile_pix)
            hg[pix, at] = (agrad[img : img + 1, at] * gp[pix, at]).astype(BF16)
        return 0

    lax.fori_loop(0, hid // HID_BLOCK, grad_block, 0)

    def back_block(c, _):
        at = pl.ds(pl.multiple_of(c * HID_BLOCK, HID_BLOCK), HID_BLOCK)
        cg[:, at] = dot_nt(hg[...], w_in[at, :])
        return 0

    lax.fori_loop(0, chan // HID_BLOCK, back_block, 0)

    wait_bytes(imgbuf.at[grp, other], sib_r.at[1])
    grp_send(imgbuf.at[grp], img_s, img_r)

    def conv_grad_rows(b, _):
        at = pl.ds(pl.multiple_of(b * ROW_BLOCK, ROW_BLOCK), ROW_BLOCK)
        grad = cg[at, :]
        normed = co[at, :]
        m1 = jnp.mean(grad, axis=-1, keepdims=True)
        m2 = jnp.mean(grad * normed, axis=-1, keepdims=True)
        cg[at, :] = inv[at, 0:1] * (grad - m1 - normed * m2)
        return 0

    lax.fori_loop(0, images * tile_pix // ROW_BLOCK, conv_grad_rows, 0)

    def tap_sums(out, tile0):
        def step(t, _):
            lanes = pl.ds(pl.multiple_of((tile0 + t) * LANES, LANES), LANES)
            for j in range(TAPS):
                sums = [jnp.zeros((cols, LANES), F32) for _ in range(TAPS)]
                for img in range(images):
                    grad = cg[img * tile_pix : (img + 1) * tile_pix, lanes]
                    moved = shift_cols(grad.reshape(rows, cols, LANES), HALF - j)
                    for i in range(TAPS):
                        sums[i] = sums[i] + jnp.sum(
                            xf[img, i : i + rows, :, lanes] * moved, axis=0
                        )
                for i in range(TAPS):
                    out[t * (TAPS * TAPS) + i * TAPS + j] = jnp.sum(
                        sums[i], axis=0, keepdims=True
                    )
            return 0

        lax.fori_loop(0, half_tiles, step, 0)

    tap_sums(ksend, half_tiles * other)
    k_sib = sib_copy(ksend.at[pl.ds(0, used)], krecv.at[pl.ds(0, used)], 2)
    k_sib.start()
    kown[pl.ds(used, n_space * chunk - used)] = jnp.zeros((n_space * chunk - used, 1, LANES), F32)
    tap_sums(kown, half_tiles * core)
    wait_bytes(krecv.at[pl.ds(0, used)], sib_r.at[2])
    kown[pl.ds(0, used)] += krecv[pl.ds(0, used)]

    space_send(lambda peer: kown.at[pl.ds(peer * chunk, chunk)], p1.at[sp], p1_s, p1_r)
    p1[sp] = kown[pl.ds(sp * chunk, chunk)]

    wait_bytes(imgbuf.at[pl.ds(0, n_grp - 1)], img_r)
    for g in range(n_grp):
        for c in range(2):
            r = (2 * g + c) * images
            img64[r : r + images, :] = imgbuf[g, c, :, 0:chan].astype(F32)
            pos64[r : r + images, :] = imgbuf[g, c, :, chan:].astype(F32)
    all_img = img64[...].astype(BF16)
    all_logits = LOGIT_SCALE * dot_nt(all_img, text_cast) + LOGIT_BIAS
    all_col = lax.broadcasted_iota(jnp.int32, (n_img, n_img), 1).astype(F32)
    all_labels = jnp.where(pos64[:, 0:n_img] == all_col, 1.0, -1.0)
    score = -all_labels * all_logits
    soft = jnp.maximum(score, 0.0) + jnp.log1p(jnp.exp(-jnp.abs(score)))
    loss_ref[...] = jnp.sum(jnp.sum(soft, axis=1, keepdims=True), axis=0, keepdims=True) / n_img
    all_pair = (-all_labels * jax.nn.sigmoid(score)).astype(BF16)
    own_col = lax.broadcasted_iota(jnp.int32, (images, n_img), 1)
    own_row = lax.broadcasted_iota(jnp.int32, (images, n_img), 0) + dp * images
    pick = jnp.where(own_col == own_row, 1.0, 0.0).astype(BF16)
    own_pair = dot_nt(pick, all_pair).astype(BF16)
    caption_side = LOGIT_SCALE * dot_nn(own_pair, all_img)
    text = captions_ref[...].astype(F32)
    text_norm = jnp.sqrt(jnp.sum(text * text, axis=-1, keepdims=True) + EPS)
    text_unit = text / text_norm
    text_grad_ref[...] = (
        caption_side - text_unit * jnp.sum(text_unit * caption_side, axis=-1, keepdims=True)
    ) / text_norm

    wait_bytes(p1.at[pl.ds(0, n_space - 1)], p1_r)
    p2[grp] = jnp.sum(p1[...], axis=0)
    grp_send(p2.at[grp], p2_s, p2_r)
    wait_bytes(p2.at[pl.ds(0, n_grp - 1)], p2_r)
    mine = kfull.at[core, pl.ds(sp * chunk, chunk)]
    kfull[core, pl.ds(sp * chunk, chunk)] = jnp.sum(p2[...], axis=0)
    space_send(lambda peer: mine, mine, p3_s, p3_r)
    wait_bytes(kfull.at[core, pl.ds(0, (n_space - 1) * chunk)], p3_r)
    full_sib = sib_copy(kfull.at[core, pl.ds(0, used)], kfull.at[core, pl.ds(0, used)], 3)
    full_sib.start()
    wait_bytes(kfull.at[other, pl.ds(0, used)], sib_r.at[3])

    def place(i, _):
        for side in range(2):
            for t in range(half_tiles):
                lane0 = (side * half_tiles + t) * LANES
                for j in range(TAPS):
                    kernel_grad_ref[i, j : j + 1, lane0 : lane0 + LANES] = kfull[
                        side, t * (TAPS * TAPS) + i * TAPS + j
                    ]
        return 0

    lax.fori_loop(0, TAPS, place, 0)

    @pl.when(jnp.logical_not(last))
    def _():
        wait_bytes(halo.at[0], halo_s.at[0])

    @pl.when(jnp.logical_not(first))
    def _():
        wait_bytes(halo.at[1], halo_s.at[1])

    wait_bytes(capbuf.at[grp, core], sib_s.at[0])
    wait_bytes(imgbuf.at[grp, core], sib_s.at[1])
    wait_bytes(ksend.at[pl.ds(0, used)], sib_s.at[2])
    wait_bytes(kfull.at[core, pl.ds(0, used)], sib_s.at[3])
    wait_bytes(capbuf.at[pl.ds(0, n_grp - 1)], cap_s)
    wait_bytes(imgbuf.at[pl.ds(0, n_grp - 1)], img_s)
    wait_bytes(pool.at[pl.ds(0, n_space - 1)], pool_s)
    wait_bytes(p1.at[pl.ds(0, n_space - 1)], p1_s)
    wait_bytes(p2.at[pl.ds(0, n_grp - 1)], p2_s)
    wait_bytes(kfull.at[core, pl.ds(0, (n_space - 1) * chunk)], p3_s)


def solution(mesh):
    n_space, n_dp = mesh.shape["space"], mesh.shape["dp"]
    n_grp = n_dp // 2

    def per_device(scenes, taps, weight_in, weight_out, captions, positives):
        images, rows, cols, chan = scenes.shape
        hid = weight_in.shape[1]
        pix = images * rows * cols
        n_img = images * n_dp
        used = chan // 2 // LANES * TAPS * TAPS
        chunk = -(-used // n_space)
        vmem = pl.BlockSpec(memory_space=pltpu.VMEM)
        hbm = pl.BlockSpec(memory_space=pl.ANY)
        dma = pltpu.SemaphoreType.DMA
        loss, text_grad, kernel_grad = pl.pallas_call(
            functools.partial(kernel, (n_space, n_dp)),
            out_shape=(
                jax.ShapeDtypeStruct((1, 1), F32),
                jax.ShapeDtypeStruct((images, chan), F32),
                jax.ShapeDtypeStruct((TAPS, TAPS, chan), F32),
            ),
            in_specs=[vmem, vmem, hbm, hbm, vmem, pl.BlockSpec(memory_space=pltpu.SMEM)],
            out_specs=(vmem, vmem, vmem),
            scratch_shapes=[
                pltpu.VMEM((images, rows + 2 * HALF, cols, chan), F32),
                pltpu.VMEM((TAPS, TAPS, chan), F32),
                pltpu.VMEM((2, images, HALF, cols, chan), BF16),
                pltpu.VMEM((pix, chan), F32),
                pltpu.VMEM((pix, chan), BF16),
                pltpu.VMEM((pix, LANES), F32),
                pltpu.VMEM((chan, hid), BF16),
                pltpu.VMEM((hid, chan), BF16),
                pltpu.VMEM((pix, hid), F32),
                pltpu.VMEM((8, hid), F32),
                pltpu.VMEM((images, chan), F32),
                pltpu.VMEM((pix, hid), BF16),
                pltpu.VMEM((pix, chan), F32),
                pltpu.VMEM((images, hid), F32),
                pltpu.VMEM((n_space, images, chan), F32),
                pltpu.VMEM((n_grp, 2, images, chan), BF16),
                pltpu.VMEM((n_img, chan), F32),
                pltpu.VMEM((n_img, chan), BF16),
                pltpu.VMEM((n_grp, 2, images, chan + LANES), BF16),
                pltpu.VMEM((n_img, chan), F32),
                pltpu.VMEM((n_img, LANES), F32),
                pltpu.VMEM((n_space * chunk, 1, LANES), F32),
                pltpu.VMEM((n_space * chunk, 1, LANES), F32),
                pltpu.VMEM((n_space * chunk, 1, LANES), F32),
                pltpu.VMEM((n_space, chunk, 1, LANES), F32),
                pltpu.VMEM((n_grp, chunk, 1, LANES), F32),
                pltpu.VMEM((2, n_space * chunk, 1, LANES), F32),
                dma((2,)), dma((2,)), dma((2,)), dma((4,)), dma((4,)),
                dma, dma, dma, dma, dma, dma, dma, dma, dma, dma, dma, dma,
            ],
            compiler_params=pltpu.CompilerParams(
                collective_id=0, has_side_effects=True, vmem_limit_bytes=48 << 20
            ),
        )(scenes, taps, weight_in, weight_out, captions, positives)
        return loss.reshape(()), text_grad, kernel_grad

    return jax.shard_map(
        per_device,
        mesh=mesh,
        in_specs=(P("dp", "space", None, None), P(), P(), P(), P("dp", None), P("dp")),
        out_specs=(P(), P("dp", None), P()),
        check_vma=False,
    )
```
